32 devices in a mesh: seq: 16 (over z, y, core), head: 2 (over x).
Axes of the slice: x: 2, y: 2, z: 4, core: 2. Of those that a mesh axis runs over, the one named last changes fastest.
Arguments:
- queries: bfloat16 [8192, 4096], P('seq', 'head'), may hold values from -20 to 20
- key_rows: bfloat16 [8192, 2048], P('seq', 'head'), may hold values from -20 to 20
- values: bfloat16 [8192, 2048], P('seq', 'head'), may hold values from -24 to 24
- out_weight: bfloat16 [4096, 5376], P('head'), may hold values from -0.09375 to 0.09375
Outputs:
- projected: bfloat16 [8192, 5376], P(('seq', 'head'))
The draws below stay inside these ranges and needn't reach their ends.
All inputs are finite; a program needn't handle non-finite values.
Results may differ from the reference program's by a relative error of at most 0.019.
Values may be sent and summed in bfloat16 or wider, within the bound.
A program may use at most 192 MiB of HBM per device.

```python
import math
import jax
import jax.numpy as jnp
from jax import lax

D = 5376
QH = 32
KVH = 16
HD = 128
TOKENS = 8192


def query_key_pair(key):
    base_key = jax.random.fold_in(key, 101)
    query_key, rows_key = jax.random.split(base_key, 2)
    queries = 1.6 * jnp.clip(jax.random.normal(query_key, (TOKENS, QH * HD), jnp.float32), -4.0, 4.0)
    key_rows = 1.6 * jnp.clip(jax.random.normal(rows_key, (TOKENS, KVH * HD), jnp.float32), -4.0, 4.0)
    return (queries, key_rows)


def draw_queries(key, part):
    return query_key_pair(key)[0].astype(jnp.bfloat16)


def draw_key_rows(key, part):
    return query_key_pair(key)[1].astype(jnp.bfloat16)


def block_levels(own_key, shape, cuts, smallest, largest):
    def one(dim, parts):
        draws = jax.random.uniform(jax.random.fold_in(jax.random.fold_in(own_key, 6), dim), (parts,), jnp.float32, smallest / len(cuts), largest / len(cuts))
        return jnp.repeat(jnp.exp(draws), shape[dim] // parts).reshape((-1,) + (1,) * (len(shape) - dim - 1))

    level = one(*cuts[0])
    for cut in cuts[1:]:
        level = level * one(*cut)
    return level


def noise(own_key, dims, spread, reach, cuts=(), kind=jnp.bfloat16):
    array = jax.random.normal(own_key, dims, jnp.float32) * spread
    if len(cuts) > 0:
        array = block_levels(own_key, dims, cuts, -0.22, 0.18) * array
    return jnp.clip(array, min=-reach, max=reach).astype(kind)


def setup_inputs(seed: int = 0) -> dict:
    arg_keys = jax.random.split(jax.random.key(seed), 5)
    return {
        "queries": draw_queries(jax.random.fold_in(arg_keys[4], 71), 0),
        "key_rows": draw_key_rows(jax.random.fold_in(arg_keys[4], 71), 0),
        "values": noise(arg_keys[2], (TOKENS, KVH * HD), 4.0, 24.0, ((0, 16), (1, 2))),
        "out_weight": noise(arg_keys[3], (QH * HD, D), (QH * HD) ** -0.5, 0.09375, ((0, 2),)),
    }


attn_scale = 168.0 ** -0.5
neg_fill = -1e30


def reference(queries, key_rows, values, out_weight):
    per_group = QH // KVH
    query_grid = queries.reshape(TOKENS, KVH, per_group, HD)
    key_grid = key_rows.reshape(TOKENS, KVH, HD)
    value_grid = values.reshape(TOKENS, KVH, HD)
    block_rows = math.gcd(TOKENS, 512)
    blocks = TOKENS // block_rows
    order_index = jnp.arange(blocks * KVH, dtype=jnp.int32)

    def one_block(index):
        block_id = (index // KVH).astype(jnp.int32)
        head_id = (index % KVH).astype(jnp.int32)
        zero = jnp.int32(0)
        query_part = lax.dynamic_slice(query_grid, (block_id * block_rows, head_id, zero, zero), (block_rows, 1, per_group, HD))[:, 0]
        key_part = lax.dynamic_slice(key_grid, (zero, head_id, zero), (TOKENS, 1, HD))[:, 0]
        value_part = lax.dynamic_slice(value_grid, (zero, head_id, zero), (TOKENS, 1, HD))[:, 0]
        scores = jnp.einsum("qgd,kd->gqk", query_part.astype(jnp.float32), key_part.astype(jnp.float32)) * attn_scale
        query_pos = block_id * block_rows + jnp.arange(block_rows, dtype=jnp.int32)
        key_pos = jnp.arange(TOKENS, dtype=jnp.int32)
        allowed = key_pos[None, :] <= query_pos[:, None]
        scores = jnp.where(allowed[None], scores, neg_fill)
        row_max = jnp.max(scores, axis=-1, keepdims=True)
        weights = jnp.where(allowed[None], jnp.exp(scores - row_max), 0.0)
        row_sum = jnp.sum(weights, axis=-1)
        rounded = weights.astype(jnp.bfloat16)
        mixed = jnp.einsum("gqk,kd->gqd", rounded.astype(jnp.float32), value_part.astype(jnp.float32))
        return (mixed / row_sum[..., None]).astype(jnp.bfloat16)

    outputs = lax.map(one_block, order_index)
    outputs = outputs.reshape(blocks, KVH, per_group, block_rows, HD)
    attended = outputs.transpose(0, 3, 1, 2, 4).reshape(TOKENS, QH * HD)
    return jnp.dot(attended, out_weight, preferred_element_type=jnp.float32).astype(jnp.bfloat16)
```

```python
import functools
import math

import jax
import jax.numpy as jnp
from jax import lax
from jax.experimental import pallas as pl
from jax.experimental.pallas import tpu as pltpu
from jax.sharding import PartitionSpec as P

HD = 128
SCALE = 168.0 ** (-0.5) * math.log2(math.e)
NEG = -1e30


def attn_kernel(span, width, parts, bq, bkv, q_ref, k_ref, v_ref, o_ref, kt, v1, m_s, acc_s):
    i = pl.program_id(0)
    total = k_ref.shape[0]
    pieces = 4
    step = bq // pieces
    sub = lax.rem(lax.axis_index("seq"), parts)

    @pl.when(i == 0)
    def _():
        @pl.loop(0, total // bkv)
        def _(b):
            rows = pl.ds(pl.multiple_of(b * bkv, bkv), bkv)
            flipped = k_ref[rows, :].T
            kt[:HD, rows] = flipped
            kt[HD:, rows] = flipped
            v1[rows, :HD] = v_ref[rows, :]
            v1[rows, HD:] = jnp.ones((bkv, HD), jnp.bfloat16)

    qf = q_ref[...].astype(jnp.float32) * SCALE
    high = qf.astype(jnp.bfloat16)
    low = (qf - high.astype(jnp.float32)).astype(jnp.bfloat16)
    q2 = jnp.concatenate([high, low], axis=1)
    m_s[...] = jnp.full_like(m_s, NEG)
    acc_s[...] = jnp.zeros_like(acc_s)

    def block(j, masked):
        cols = pl.ds(pl.multiple_of(j * bkv, bkv), bkv)
        for t in range(pieces):
            rows = slice(t * step, (t + 1) * step)
            s = jnp.dot(q2[rows], kt[:, cols], preferred_element_type=jnp.float32)
            if masked:
                row = i * bq + t * step + lax.broadcasted_iota(jnp.int32, (step, 1), 0)
                pos = (row // width) * span + sub * width + row % width
                col = j * bkv + lax.broadcasted_iota(jnp.int32, (1, bkv), 1)
                s = jnp.where(col <= pos, s, NEG)
            m0 = m_s[rows, :]
            m1 = jnp.maximum(m0, jnp.max(s, axis=1, keepdims=True))
            m_s[rows, :] = m1
            p = jnp.exp2(s - jnp.tile(m1, (1, bkv // HD))).astype(jnp.bfloat16)
            f = jnp.exp2(m0 - m1)
            acc_s[rows, :] = acc_s[rows, :] * jnp.tile(f, (1, 2)) + jnp.dot(
                p, v1[cols, :], preferred_element_type=jnp.float32
            )

    full = ((i * bq // width) * span + sub * width + 1) // bkv
    last = (((i + 1) * bq // width - 1) * span + sub * width + width - 1) // bkv + 1

    def one(masked, j, c):
        block(j, masked)
        return c

    lax.fori_loop(0, full, functools.partial(one, False), 0)
    lax.fori_loop(full, last, functools.partial(one, True), 0)
    a = acc_s[...]
    o_ref[...] = (a[:, :HD] / a[:, HD:]).astype(o_ref.dtype)


def attention(q, k, v, span, width, parts):
    rows, total = q.shape[0], k.shape[0]
    bq = math.gcd(rows, 1024)
    bkv = math.gcd(total, 1024)
    return pl.pallas_call(
        functools.partial(attn_kernel, span, width, parts, bq, bkv),
        grid=(rows // bq,),
        in_specs=[
            pl.BlockSpec((bq, HD), lambda i: (i, 0)),
            pl.BlockSpec((total, HD), lambda i: (0, 0)),
            pl.BlockSpec((total, HD), lambda i: (0, 0)),
        ],
        out_specs=pl.BlockSpec((bq, HD), lambda i: (i, 0)),
        out_shape=jax.ShapeDtypeStruct((rows, HD), jnp.bfloat16),
        scratch_shapes=[
            pltpu.VMEM((2 * HD, total), jnp.bfloat16),
            pltpu.VMEM((total, 2 * HD), jnp.bfloat16),
            pltpu.VMEM((bq, HD), jnp.float32),
            pltpu.VMEM((bq, 2 * HD), jnp.float32),
        ],
        compiler_params=pltpu.CompilerParams(vmem_limit_bytes=60 * 2**20),
    )(q, k, v)


def per_device(queries, key_rows, values, out_weight):
    n = lax.axis_size("seq")
    heads = lax.axis_size("head")
    mine = lax.axis_index("head")
    span = queries.shape[0]
    qh = queries.shape[1] // HD
    kvh = key_rows.shape[1] // HD
    parts = n // qh
    width = span // parts
    q = queries.reshape(parts, width, qh, HD).transpose(2, 0, 1, 3).reshape(n, width, HD)

    def spread(x):
        x = x.reshape(span, kvh, HD).transpose(1, 0, 2)
        x = jnp.repeat(x, n // kvh, axis=0)
        return lax.all_to_all(x, "seq", 0, 0, tiled=True).reshape(n * span, HD)

    q = lax.all_to_all(q, "seq", 0, 0, tiled=True).reshape(n * width, HD)
    out = attention(q, spread(key_rows), spread(values), span, width, parts)
    out = lax.all_to_all(out.reshape(n, width, HD), "seq", 0, 0, tiled=True)
    attended = out.reshape(qh, parts, width, HD).transpose(1, 2, 0, 3).reshape(span, qh * HD)
    return lax.psum_scatter(
        jnp.dot(attended, out_weight, preferred_element_type=jnp.float32).astype(jnp.bfloat16),
        "head",
        scatter_dimension=0,
        tiled=True,
    )


def solution(mesh):
    placed = (P("seq", "head"), P("seq", "head"), P("seq", "head"), P("head", None))
    return jax.shard_map(
        per_device, mesh=mesh, in_specs=placed, out_specs=P(("seq", "head"), None), check_vma=False
    )
```

```python
import functools
import math

import jax
import jax.numpy as jnp
from jax import lax
from jax.experimental import pallas as pl
from jax.experimental.pallas import tpu as pltpu
from jax.sharding import PartitionSpec as P

HD = 128
SCALE = 168.0 ** (-0.5) * math.log2(math.e)
NEG = -1e30


def attn_kernel(span, width, parts, bq, bkv, q_ref, k_ref, v_ref, o_ref, kt, v1, m_s, acc_s):
    i = pl.program_id(0)
    total = k_ref.shape[0]
    pieces = 4
    step = bq // pieces
    sub = lax.rem(lax.axis_index("seq"), parts)

    @pl.when(i == 0)
    def _():
        @pl.loop(0, total // bkv)
        def _(b):
            rows = pl.ds(pl.multiple_of(b * bkv, bkv), bkv)
            flipped = k_ref[rows, :].T
            kt[:HD, rows] = flipped
            kt[HD:, rows] = flipped
            v1[rows, :HD] = v_ref[rows, :]
            v1[rows, HD:] = jnp.ones((bkv, HD), jnp.bfloat16)

    qf = q_ref[...].astype(jnp.float32) * SCALE
    high = qf.astype(jnp.bfloat16)
    low = (qf - high.astype(jnp.float32)).astype(jnp.bfloat16)
    q2 = jnp.concatenate([high, low], axis=1)
    m_s[...] = jnp.full_like(m_s, NEG)
    acc_s[...] = jnp.zeros_like(acc_s)

    def block(j, masked):
        cols = pl.ds(pl.multiple_of(j * bkv, bkv), bkv)
        for t in range(pieces):
            rows = slice(t * step, (t + 1) * step)
            s = jnp.dot(q2[rows], kt[:, cols], preferred_element_type=jnp.float32)
            if masked:
                row = i * bq + t * step + lax.broadcasted_iota(jnp.int32, (step, 1), 0)
                pos = (row // width) * span + sub * width + row % width
                col = j * bkv + lax.broadcasted_iota(jnp.int32, (1, bkv), 1)
                s = jnp.where(col <= pos, s, NEG)
            m0 = m_s[rows, :]
            m1 = jnp.maximum(m0, jnp.max(s, axis=1, keepdims=True))
            m_s[rows, :] = m1
            p = jnp.exp2(s - jnp.tile(m1, (1, bkv // HD))).astype(jnp.bfloat16)
            f = jnp.exp2(m0 - m1)
            acc_s[rows, :] = acc_s[rows, :] * jnp.tile(f, (1, 2)) + jnp.dot(
                p, v1[cols, :], preferred_element_type=jnp.float32
            )

    full = ((i * bq // width) * span + sub * width + 1) // bkv
    last = (((i + 1) * bq // width - 1) * span + sub * width + width - 1) // bkv + 1

    def one(masked, j, c):
        block(j, masked)
        return c

    lax.fori_loop(0, full, functools.partial(one, False), 0)
    lax.fori_loop(full, last, functools.partial(one, True), 0)
    a = acc_s[...]
    o_ref[...] = (a[:, :HD] / a[:, HD:]).astype(o_ref.dtype)


def attention(q, k, v, span, width, parts):
    rows, total = q.shape[0], k.shape[0]
    bq = math.gcd(rows, 1024)
    bkv = math.gcd(total, 1024)
    return pl.pallas_call(
        functools.partial(attn_kernel, span, width, parts, bq, bkv),
        grid=(rows // bq,),
        in_specs=[
            pl.BlockSpec((bq, HD), lambda i: (i, 0)),
            pl.BlockSpec((total, HD), lambda i: (0, 0)),
            pl.BlockSpec((total, HD), lambda i: (0, 0)),
        ],
        out_specs=pl.BlockSpec((bq, HD), lambda i: (i, 0)),
        out_shape=jax.ShapeDtypeStruct((rows, HD), jnp.bfloat16),
        scratch_shapes=[
            pltpu.VMEM((2 * HD, total), jnp.bfloat16),
            pltpu.VMEM((total, 2 * HD), jnp.bfloat16),
            pltpu.VMEM((bq, HD), jnp.float32),
            pltpu.VMEM((bq, 2 * HD), jnp.float32),
        ],
        compiler_params=pltpu.CompilerParams(vmem_limit_bytes=60 * 2**20),
    )(q, k, v)


MESH = pl.DeviceIdType.MESH


def greet(n):
    me = lax.axis_index("seq")
    barrier = pltpu.get_barrier_semaphore()

    @pl.loop(1, n)
    def _(d):
        pl.semaphore_signal(
            barrier, inc=1, device_id={"seq": lax.rem(me + d, n)}, device_id_type=MESH
        )

    pl.semaphore_wait(barrier, n - 1)
    return me


def remote(src, dst, send, recv, peer):
    return pltpu.make_async_remote_copy(
        src_ref=src,
        dst_ref=dst,
        send_sem=send,
        recv_sem=recv,
        device_id={"seq": peer},
        device_id_type=MESH,
    )


def inbound(n, parts, width, dup, q_ref, k_ref, v_ref, q_o, k_o, v_o, send, recv, own, send2, recv2):
    me = greet(n)
    span = q_ref.shape[0]
    frac = span // dup

    def sources(j):
        head = j // parts
        rows = pl.ds(pl.multiple_of(lax.rem(j, parts) * width, width), width)
        q = q_ref.at[rows, pl.ds(pl.multiple_of(head * HD, HD), HD)]
        kv_rows = pl.ds(pl.multiple_of(lax.rem(j, dup) * frac, frac), frac)
        kv_cols = pl.ds(pl.multiple_of(j // dup * HD, HD), HD)
        return q, k_ref.at[kv_rows, kv_cols], v_ref.at[kv_rows, kv_cols]

    def places(owner, j):
        kv_rows = pl.ds(pl.multiple_of(lax.rem(j, dup) * frac, frac), frac)
        return q_o.at[owner], k_o.at[owner, kv_rows], v_o.at[owner, kv_rows]

    def copies(d):
        peer = lax.rem(me + d, n)
        pairs = zip(sources(peer), places(me, peer))
        return [remote(x, y, send.at[i, d], recv.at[i, d], peer) for i, (x, y) in enumerate(pairs)]

    @pl.loop(1, n)
    def _(d):
        for i in (1, 2, 0):
            copies(d)[i].start()

    local = [
        pltpu.make_async_copy(x, y, own.at[i])
        for i, (x, y) in enumerate(zip(sources(me), places(me, me)))
    ]
    for c in local:
        c.start()
    for c in local:
        c.wait()

    def arrived(i):
        @pl.loop(1, n)
        def _(d):
            owner = lax.rem(me + n - d, n)
            place = places(owner, me)[i]
            remote(place, place, send.at[i, d], recv.at[i, d], owner).wait_recv()

    arrived(1)
    arrived(2)
    base = me // dup * dup
    mine = lax.rem(me, dup)

    def shares(d):
        peer = base + lax.rem(mine + d, dup)
        rows = pl.ds(pl.multiple_of(mine * frac, frac), frac)
        return [
            remote(x.at[:, rows], x.at[:, rows], send2.at[i, d], recv2.at[i, d], peer)
            for i, x in enumerate((k_o, v_o))
        ]

    for d in range(1, dup):
        for c in shares(d):
            c.start()
    arrived(0)
    for d in range(1, dup):
        owner = lax.rem(mine + dup - d, dup)
        rows = pl.ds(pl.multiple_of(owner * frac, frac), frac)
        for i, x in enumerate((k_o, v_o)):
            place = x.at[:, rows]
            remote(place, place, send2.at[i, d], recv2.at[i, d], base + owner).wait_recv()
        for c in shares(d):
            c.wait_send()

    @pl.loop(1, n)
    def _(d):
        for c in copies(d):
            c.wait_send()


def gather_heads(q, k, v, n, parts, width, dup):
    span = q.shape[0]
    any_space = pl.BlockSpec(memory_space=pl.ANY)
    vmem = pl.BlockSpec(memory_space=pltpu.VMEM)
    return pl.pallas_call(
        functools.partial(inbound, n, parts, width, dup),
        in_specs=[any_space] * 3,
        out_specs=[vmem] * 3,
        out_shape=[
            jax.ShapeDtypeStruct((n, width, HD), jnp.bfloat16),
            jax.ShapeDtypeStruct((n, span, HD), jnp.bfloat16),
            jax.ShapeDtypeStruct((n, span, HD), jnp.bfloat16),
        ],
        scratch_shapes=[
            pltpu.SemaphoreType.DMA((3, n)),
            pltpu.SemaphoreType.DMA((3, n)),
            pltpu.SemaphoreType.DMA((3,)),
            pltpu.SemaphoreType.DMA((2, dup)),
            pltpu.SemaphoreType.DMA((2, dup)),
        ],
        compiler_params=pltpu.CompilerParams(
            collective_id=0, has_side_effects=True, vmem_limit_bytes=40 * 2**20
        ),
    )(q, k, v)


def outbound(n, parts, width, x_ref, o_ref, send, recv, own):
    me = greet(n)

    def place(j):
        rows = pl.ds(pl.multiple_of(lax.rem(j, parts) * width, width), width)
        return o_ref.at[rows, pl.ds(pl.multiple_of(j // parts * HD, HD), HD)]

    def copy(d):
        peer = lax.rem(me + d, n)
        return remote(x_ref.at[peer], place(me), send.at[d], recv.at[d], peer)

    @pl.loop(1, n)
    def _(d):
        copy(d).start()

    local = pltpu.make_async_copy(x_ref.at[me], place(me), own)
    local.start()
    local.wait()

    @pl.loop(1, n)
    def _(d):
        owner = lax.rem(me + n - d, n)
        there = place(owner)
        remote(there, there, send.at[d], recv.at[d], owner).wait_recv()
        copy(d).wait_send()


def return_heads(x, n, parts, width, span, qh):
    return pl.pallas_call(
        functools.partial(outbound, n, parts, width),
        in_specs=[pl.BlockSpec(memory_space=pl.ANY)],
        out_specs=pl.BlockSpec(memory_space=pltpu.VMEM),
        out_shape=jax.ShapeDtypeStruct((span, qh * HD), jnp.bfloat16),
        scratch_shapes=[
            pltpu.SemaphoreType.DMA((n,)),
            pltpu.SemaphoreType.DMA((n,)),
            pltpu.SemaphoreType.DMA,
        ],
        compiler_params=pltpu.CompilerParams(
            collective_id=1, has_side_effects=True, vmem_limit_bytes=40 * 2**20
        ),
    )(x)


def project(attended, out_weight):
    heads = lax.axis_size("head")
    mine = lax.axis_index("head")
    rows = attended.shape[0] // heads
    columns = out_weight.shape[1]
    chunks = next(c for c in (6, 4, 3, 2, 1) if columns % (c * HD) == 0)
    step = columns // chunks

    def part(dest, c):
        x = lax.dynamic_slice_in_dim(attended, dest * rows, rows, 0)
        w = out_weight[:, c * step : (c + 1) * step]
        return jnp.dot(x, w, preferred_element_type=jnp.float32)

    done = []
    received = []
    for c in range(chunks):
        got = []
        for k in range(1, heads):
            term = part(lax.rem(mine + k, heads), c).astype(jnp.bfloat16)
            got.append(lax.ppermute(term, "head", [(i, (i + k) % heads) for i in range(heads)]))
        received.append(got)
    for c in range(chunks):
        total = part(mine, c)
        for got in received[c]:
            total = total + got.astype(jnp.float32)
        done.append(total.astype(jnp.bfloat16))
    return jnp.concatenate(done, axis=1)


def per_device(queries, key_rows, values, out_weight):
    n = lax.axis_size("seq")
    span = queries.shape[0]
    qh = queries.shape[1] // HD
    kvh = key_rows.shape[1] // HD
    parts = n // qh
    width = span // parts
    q, k, v = gather_heads(queries, key_rows, values, n, parts, width, n // kvh)
    q = q.reshape(n * width, HD)
    out = attention(q, k.reshape(n * span, HD), v.reshape(n * span, HD), span, width, parts)
    attended = return_heads(out.reshape(n, width, HD), n, parts, width, span, qh)
    return project(attended, out_weight)


def solution(mesh):
    placed = (P("seq", "head"), P("seq", "head"), P("seq", "head"), P("head", None))
    return jax.shard_map(
        per_device, mesh=mesh, in_specs=placed, out_specs=P(("seq", "head"), None), check_vma=False
    )
```

```python
import functools
import math

import jax
import jax.numpy as jnp
from jax import lax
from jax.experimental import pallas as pl
from jax.experimental.pallas import tpu as pltpu
from jax.sharding import PartitionSpec as P

HD = 128
SCALE = 168.0 ** (-0.5) * math.log2(math.e)
NEG = -1e30


def attn_body(lay, phase, q_ref, k_ref, v_ref, o_ref, kt, v1, m_s, acc_s):
    n, parts, runs, run_rows, ph, span = lay
    total = k_ref.shape[0]
    rows_each = runs * ph
    count = q_ref.shape[0]
    bq = math.gcd(count, 1024)
    bkv = math.gcd(total, 1024)
    pieces = 4
    step = bq // pieces
    sub = lax.rem(lax.axis_index("seq"), parts)
    reach = bq // rows_each * span

    @pl.loop(0, total // bkv)
    def _(b):
        rows = pl.ds(pl.multiple_of(b * bkv, bkv), bkv)
        flipped = k_ref[rows, :].T
        kt[:HD, rows] = flipped
        kt[HD:, rows] = flipped
        v1[rows, :HD] = v_ref[rows, :]
        v1[rows, HD:] = jnp.ones((bkv, HD), jnp.bfloat16)

    @pl.loop(0, count // bq)
    def _(i):
        here = pl.ds(pl.multiple_of(i * bq, bq), bq)
        qf = q_ref[here, :].astype(jnp.float32) * SCALE
        high = qf.astype(jnp.bfloat16)
        low = (qf - high.astype(jnp.float32)).astype(jnp.bfloat16)
        q2 = jnp.concatenate([high, low], axis=1)
        m_s[...] = jnp.full_like(m_s, NEG)
        acc_s[...] = jnp.zeros_like(acc_s)

        def piece(t, start, masked):
            cols = pl.ds(pl.multiple_of(start, bkv), bkv)
            rows = slice(t * step, (t + 1) * step)
            s = jnp.dot(q2[rows], kt[:, cols], preferred_element_type=jnp.float32)
            if masked:
                row = i * bq + t * step + lax.broadcasted_iota(jnp.int32, (step, 1), 0)
                run = sub * runs + row // ph % runs
                pos = row // rows_each * span + run * run_rows + phase * ph + row % ph
                col = start + lax.broadcasted_iota(jnp.int32, (1, bkv), 1)
                s = jnp.where(col <= pos, s, NEG)
            m0 = m_s[rows, :]
            m1 = jnp.maximum(m0, jnp.max(s, axis=1, keepdims=True))
            m_s[rows, :] = m1
            p = jnp.exp2(s - jnp.tile(m1, (1, bkv // HD))).astype(jnp.bfloat16)
            f = jnp.exp2(m0 - m1)
            acc_s[rows, :] = acc_s[rows, :] * jnp.tile(f, (1, 2)) + jnp.dot(
                p, v1[cols, :], preferred_element_type=jnp.float32
            )

        def whole(j, c):
            for t in range(pieces):
                piece(t, j * bkv, False)
            return c

        lax.fori_loop(0, i * (reach // bkv), whole, 0)
        for j in range(reach // bkv):
            for t in range(pieces):
                first = t * step // rows_each * span
                last = (((t + 1) * step - 1) // rows_each + 1) * span
                if j * bkv < last:
                    piece(t, i * reach + j * bkv, first < (j + 1) * bkv)
        out = acc_s[...]
        o_ref[here, :] = (out[:, :HD] / out[:, HD:]).astype(o_ref.dtype)


def query_source(lay, x, phase, j):
    n, parts, runs, run_rows, ph, span = lay
    return x.at[
        pl.ds(lax.rem(j, parts) * runs, runs),
        pl.ds(phase * ph, ph),
        pl.ds(pl.multiple_of(j // parts * HD, HD), HD),
    ]


def head_place(lay, x, j):
    n, parts, runs, run_rows, ph, span = lay
    return x.at[
        pl.ds(lax.rem(j, parts) * runs, runs),
        slice(None),
        pl.ds(pl.multiple_of(j // parts * HD, HD), HD),
    ]


def attn_kernel(lay, phase, carry, q_ref, k_ref, v_ref, x_ref, o_ref, y_ref, kt, v1, m_s, acc_s, *sems):
    n = lay[0]
    me = greet(n)
    if carry == "queries":
        exchange = (lambda j: query_source(lay, x_ref, phase + 1, j)), (lambda j: y_ref.at[j])
    else:
        exchange = (lambda j: x_ref.at[j]), (lambda j: head_place(lay, y_ref, j))
    begin_exchange(n, me, *exchange, *sems)
    attn_body(lay, phase, q_ref, k_ref, v_ref, o_ref, kt, v1, m_s, acc_s)
    end_exchange(n, me, *exchange, *sems)


def attention(lay, phase, carry, q, k, v, x, y_shape):
    n, parts, runs, run_rows, ph, span = lay
    rows, total = q.shape[0], k.shape[0]
    bq = math.gcd(rows, 1024)
    vmem = pl.BlockSpec(memory_space=pltpu.VMEM)
    return pl.pallas_call(
        functools.partial(attn_kernel, lay, phase, carry),
        in_specs=[vmem, vmem, vmem, pl.BlockSpec(memory_space=pl.ANY)],
        out_specs=[vmem, vmem],
        out_shape=[
            jax.ShapeDtypeStruct((rows, HD), jnp.bfloat16),
            jax.ShapeDtypeStruct(y_shape, jnp.bfloat16),
        ],
        scratch_shapes=[
            pltpu.VMEM((2 * HD, total), jnp.bfloat16),
            pltpu.VMEM((total, 2 * HD), jnp.bfloat16),
            pltpu.VMEM((bq, HD), jnp.float32),
            pltpu.VMEM((bq, 2 * HD), jnp.float32),
            pltpu.SemaphoreType.DMA((n,)),
            pltpu.SemaphoreType.DMA((n,)),
            pltpu.SemaphoreType.DMA,
        ],
        compiler_params=pltpu.CompilerParams(
            collective_id=2 + phase, has_side_effects=True, vmem_limit_bytes=50 * 2**20
        ),
    )(q, k, v, x)


MESH = pl.DeviceIdType.MESH


def greet(n, others=0):
    me = lax.axis_index("seq")
    barrier = pltpu.get_barrier_semaphore()

    @pl.loop(1, n)
    def _(d):
        pl.semaphore_signal(
            barrier, inc=1, device_id={"seq": lax.rem(me + d, n)}, device_id_type=MESH
        )

    pl.semaphore_wait(barrier, n - 1 + others)
    return me


def remote(src, dst, send, recv, peer):
    return pltpu.make_async_remote_copy(
        src_ref=src,
        dst_ref=dst,
        send_sem=send,
        recv_sem=recv,
        device_id={"seq": peer},
        device_id_type=MESH,
    )


def inbound(lay, dup, q_ref, k_ref, v_ref, q_o, k_o, v_o, send, recv, own, send2, recv2):
    n, parts, runs, run_rows, ph, span = lay
    me = greet(n)
    frac = span // dup

    def sources(j):
        q = query_source(lay, q_ref, 0, j)
        kv_rows = pl.ds(pl.multiple_of(lax.rem(j, dup) * frac, frac), frac)
        kv_cols = pl.ds(pl.multiple_of(j // dup * HD, HD), HD)
        return q, k_ref.at[kv_rows, kv_cols], v_ref.at[kv_rows, kv_cols]

    def places(owner, j):
        kv_rows = pl.ds(pl.multiple_of(lax.rem(j, dup) * frac, frac), frac)
        return q_o.at[owner], k_o.at[owner, kv_rows], v_o.at[owner, kv_rows]

    def copies(d):
        peer = lax.rem(me + d, n)
        pairs = zip(sources(peer), places(me, peer))
        return [remote(x, y, send.at[i, d], recv.at[i, d], peer) for i, (x, y) in enumerate(pairs)]

    @pl.loop(1, n)
    def _(d):
        for i in (1, 2, 0):
            copies(d)[i].start()

    local = [
        pltpu.make_async_copy(x, y, own.at[i])
        for i, (x, y) in enumerate(zip(sources(me), places(me, me)))
    ]
    for c in local:
        c.start()
    for c in local:
        c.wait()

    def arrived(i):
        @pl.loop(1, n)
        def _(d):
            owner = lax.rem(me + n - d, n)
            place = places(owner, me)[i]
            remote(place, place, send.at[i, d], recv.at[i, d], owner).wait_recv()

    arrived(1)
    arrived(2)
    base = me // dup * dup
    mine = lax.rem(me, dup)

    def shares(d):
        peer = base + lax.rem(mine + d, dup)
        rows = pl.ds(pl.multiple_of(mine * frac, frac), frac)
        return [
            remote(x.at[:, rows], x.at[:, rows], send2.at[i, d], recv2.at[i, d], peer)
            for i, x in enumerate((k_o, v_o))
        ]

    for d in range(1, dup):
        for c in shares(d):
            c.start()
    arrived(0)
    for d in range(1, dup):
        owner = lax.rem(mine + dup - d, dup)
        rows = pl.ds(pl.multiple_of(owner * frac, frac), frac)
        for i, x in enumerate((k_o, v_o)):
            place = x.at[:, rows]
            remote(place, place, send2.at[i, d], recv2.at[i, d], base + owner).wait_recv()
        for c in shares(d):
            c.wait_send()

    @pl.loop(1, n)
    def _(d):
        for c in copies(d):
            c.wait_send()


def gather_heads(lay, q, k, v, dup):
    n, parts, runs, run_rows, ph, span = lay
    any_space = pl.BlockSpec(memory_space=pl.ANY)
    vmem = pl.BlockSpec(memory_space=pltpu.VMEM)
    return pl.pallas_call(
        functools.partial(inbound, lay, dup),
        in_specs=[any_space] * 3,
        out_specs=[vmem] * 3,
        out_shape=[
            jax.ShapeDtypeStruct((n, runs, ph, HD), jnp.bfloat16),
            jax.ShapeDtypeStruct((n, span, HD), jnp.bfloat16),
            jax.ShapeDtypeStruct((n, span, HD), jnp.bfloat16),
        ],
        scratch_shapes=[
            pltpu.SemaphoreType.DMA((3, n)),
            pltpu.SemaphoreType.DMA((3, n)),
            pltpu.SemaphoreType.DMA((3,)),
            pltpu.SemaphoreType.DMA((2, dup)),
            pltpu.SemaphoreType.DMA((2, dup)),
        ],
        compiler_params=pltpu.CompilerParams(
            collective_id=0, has_side_effects=True, vmem_limit_bytes=40 * 2**20
        ),
    )(q, k, v)


def begin_exchange(n, me, source, place, send, recv, own):
    @pl.loop(1, n)
    def _(d):
        peer = lax.rem(me + d, n)
        remote(source(peer), place(me), send.at[d], recv.at[d], peer).start()

    pltpu.make_async_copy(source(me), place(me), own).start()


def end_exchange(n, me, source, place, send, recv, own):
    pltpu.make_async_copy(source(me), place(me), own).wait()

    @pl.loop(1, n)
    def _(d):
        owner = lax.rem(me + n - d, n)
        peer = lax.rem(me + d, n)
        there = place(owner)
        remote(there, there, send.at[d], recv.at[d], owner).wait_recv()
        remote(source(peer), place(me), send.at[d], recv.at[d], peer).wait_send()


def outbound(lay, heads, x_ref, t_ref, o_ref, g_ref, send, recv, own, send_x, recv_x):
    n = lay[0]
    mine = lax.axis_index("head")
    barrier = pltpu.get_barrier_semaphore()
    for k in range(1, heads):
        pl.semaphore_signal(
            barrier, inc=1, device_id={"head": lax.rem(mine + k, heads)}, device_id_type=MESH
        )
    me = greet(n, heads - 1)

    def term(k):
        return pltpu.make_async_remote_copy(
            src_ref=t_ref.at[k - 1],
            dst_ref=g_ref.at[k - 1],
            send_sem=send_x.at[k],
            recv_sem=recv_x.at[k],
            device_id={"head": lax.rem(mine + k, heads)},
            device_id_type=MESH,
        )

    exchange = (lambda j: x_ref.at[j]), (lambda j: head_place(lay, o_ref, j))
    for k in range(1, heads):
        term(k).start()
    begin_exchange(n, me, *exchange, send, recv, own)
    end_exchange(n, me, *exchange, send, recv, own)
    for k in range(1, heads):
        term(k).wait()


def return_heads(lay, x, shape, terms):
    n = lay[0]
    heads = lax.axis_size("head")
    space = pl.BlockSpec(memory_space=pl.ANY)
    return pl.pallas_call(
        functools.partial(outbound, lay, heads),
        in_specs=[space, space],
        out_specs=[pl.BlockSpec(memory_space=pltpu.VMEM), space],
        out_shape=[
            jax.ShapeDtypeStruct(shape, jnp.bfloat16),
            jax.ShapeDtypeStruct(terms.shape, jnp.bfloat16),
        ],
        scratch_shapes=[
            pltpu.SemaphoreType.DMA((n,)),
            pltpu.SemaphoreType.DMA((n,)),
            pltpu.SemaphoreType.DMA,
            pltpu.SemaphoreType.DMA((heads,)),
            pltpu.SemaphoreType.DMA((heads,)),
        ],
        compiler_params=pltpu.CompilerParams(
            collective_id=1, has_side_effects=True, vmem_limit_bytes=40 * 2**20
        ),
    )(x, terms)


def dot_rows(attended, out_weight, dest, columns):
    rows = attended.shape[0] // lax.axis_size("head")
    x = lax.dynamic_slice_in_dim(attended, dest * rows, rows, 0)
    return jnp.dot(x, out_weight[:, columns], preferred_element_type=jnp.float32)


def peer_terms(attended, out_weight, columns):
    heads = lax.axis_size("head")
    mine = lax.axis_index("head")
    return [
        dot_rows(attended, out_weight, lax.rem(mine + k, heads), columns).astype(jnp.bfloat16)
        for k in range(1, heads)
    ]


def project_end(attended, out_weight, columns, got):
    total = dot_rows(attended, out_weight, lax.axis_index("head"), columns)
    for term in got:
        total = total + term.astype(jnp.float32)
    return total.astype(jnp.bfloat16)


def project_last(attended, out_weight, chunks):
    heads = lax.axis_size("head")
    step = out_weight.shape[1] // chunks
    cuts = [slice(c * step, (c + 1) * step) for c in range(chunks)]
    received = [
        [
            lax.ppermute(term, "head", [(i, (i + k) % heads) for i in range(heads)])
            for k, term in enumerate(peer_terms(attended, out_weight, cut), 1)
        ]
        for cut in cuts
    ]
    done = [project_end(attended, out_weight, cut, got) for cut, got in zip(cuts, received)]
    return jnp.concatenate(done, axis=1)


def per_device(queries, key_rows, values, out_weight):
    n = lax.axis_size("seq")
    heads = lax.axis_size("head")
    span = queries.shape[0]
    qh = queries.shape[1] // HD
    kvh = key_rows.shape[1] // HD
    parts = n // qh
    runs = max(1, heads // parts)
    groups = parts * runs
    run_rows = span // groups
    phases = 2
    ph = run_rows // phases
    lay = (n, parts, runs, run_rows, ph, span)
    columns = out_weight.shape[1]
    chunks = 3 if columns % (3 * HD) == 0 else 1
    grid = queries.reshape(groups, run_rows, qh * HD)
    q0, k, v = gather_heads(lay, grid, key_rows, values, n // kvh)
    k = k.reshape(n * span, HD)
    v = v.reshape(n * span, HD)
    own = (n, runs, ph, HD)
    back = (groups, ph, qh * HD)
    out0, q1 = attention(lay, 0, "queries", q0.reshape(-1, HD), k, v, grid, own)
    out1, att0 = attention(lay, 1, "heads", q1.reshape(-1, HD), k, v, out0.reshape(own), back)
    att0 = att0.reshape(groups * ph, qh * HD)
    every = slice(0, columns)
    terms = jnp.stack(peer_terms(att0, out_weight, every))
    att1, got = return_heads(lay, out1.reshape(own), back, terms)
    second = project_last(att1.reshape(groups * ph, qh * HD), out_weight, chunks)
    first = project_end(att0, out_weight, every, [got[k] for k in range(heads - 1)])
    ends = [x.reshape(groups // heads, 1, ph, columns) for x in (first, second)]
    return jnp.concatenate(ends, axis=1).reshape(span // heads, columns)


def solution(mesh):
    placed = (P("seq", "head"), P("seq", "head"), P("seq", "head"), P("head", None))
    return jax.shard_map(
        per_device, mesh=mesh, in_specs=placed, out_specs=P(("seq", "head"), None), check_vma=False
    )
```

```python
import functools
import math

import jax
import jax.numpy as jnp
from jax import lax
from jax.experimental import pallas as pl
from jax.experimental.pallas import tpu as pltpu
from jax.sharding import PartitionSpec as P

HD = 128
SCALE = 168.0 ** (-0.5) * math.log2(math.e)
NEG = -1e30


def attn_body(lay, phase, q_ref, k_ref, v_ref, o_ref, kt, v1, m_s, acc_s):
    n, parts, runs, run_rows, ph, span = lay
    total = k_ref.shape[0]
    rows_each = runs * ph
    count = q_ref.shape[0]
    bq = math.gcd(count, 1024)
    bkv = math.gcd(total, 1024)
    pieces = 4
    step = bq // pieces
    sub = lax.rem(lax.axis_index("seq"), parts)
    reach = bq // rows_each * span

    @pl.loop(0, total // bkv)
    def _(b):
        rows = pl.ds(pl.multiple_of(b * bkv, bkv), bkv)
        flipped = k_ref[rows, :].T
        kt[:HD, rows] = flipped
        kt[HD:, rows] = flipped
        v1[rows, :HD] = v_ref[rows, :]
        v1[rows, HD:] = jnp.ones((bkv, HD), jnp.bfloat16)

    @pl.loop(0, count // bq)
    def _(i):
        here = pl.ds(pl.multiple_of(i * bq, bq), bq)
        qf = q_ref[here, :].astype(jnp.float32) * SCALE
        high = qf.astype(jnp.bfloat16)
        low = (qf - high.astype(jnp.float32)).astype(jnp.bfloat16)
        q2 = jnp.concatenate([high, low], axis=1)
        m_s[...] = jnp.full_like(m_s, NEG)
        acc_s[...] = jnp.zeros_like(acc_s)

        def piece(t, start, masked):
            cols = pl.ds(pl.multiple_of(start, bkv), bkv)
            rows = slice(t * step, (t + 1) * step)
            s = jnp.dot(q2[rows], kt[:, cols], preferred_element_type=jnp.float32)
            if masked:
                row = i * bq + t * step + lax.broadcasted_iota(jnp.int32, (step, 1), 0)
                run = sub * runs + row // ph % runs
                pos = row // rows_each * span + run * run_rows + phase * ph + row % ph
                col = start + lax.broadcasted_iota(jnp.int32, (1, bkv), 1)
                s = jnp.where(col <= pos, s, NEG)
            m0 = m_s[rows, :]
            m1 = jnp.maximum(m0, jnp.max(s, axis=1, keepdims=True))
            m_s[rows, :] = m1
            p = jnp.exp2(s - jnp.tile(m1, (1, bkv // HD))).astype(jnp.bfloat16)
            f = jnp.exp2(m0 - m1)
            acc_s[rows, :] = acc_s[rows, :] * jnp.tile(f, (1, 2)) + jnp.dot(
                p, v1[cols, :], preferred_element_type=jnp.float32
            )

        def whole(j, c):
            for t in range(pieces):
                piece(t, j * bkv, False)
            return c

        lax.fori_loop(0, i * (reach // bkv), whole, 0)
        for j in range(reach // bkv):
            for t in range(pieces):
                first = t * step // rows_each * span
                last = (((t + 1) * step - 1) // rows_each + 1) * span
                if j * bkv < last:
                    piece(t, i * reach + j * bkv, first < (j + 1) * bkv)
        out = acc_s[...]
        o_ref[here, :] = (out[:, :HD] / out[:, HD:]).astype(o_ref.dtype)


def query_source(lay, x, phase, j):
    n, parts, runs, run_rows, ph, span = lay
    return x.at[
        pl.ds(lax.rem(j, parts) * runs, runs),
        pl.ds(phase * ph, ph),
        pl.ds(pl.multiple_of(j // parts * HD, HD), HD),
    ]


def head_place(lay, x, j):
    n, parts, runs, run_rows, ph, span = lay
    return x.at[
        pl.ds(lax.rem(j, parts) * runs, runs),
        slice(None),
        pl.ds(pl.multiple_of(j // parts * HD, HD), HD),
    ]


def attn_kernel(lay, phase, carry, q_ref, k_ref, v_ref, x_ref, o_ref, y_ref, kt, v1, m_s, acc_s, *sems):
    n = lay[0]
    me = greet(n)
    if carry == "queries":
        exchange = (lambda j: query_source(lay, x_ref, phase + 1, j)), (lambda j: y_ref.at[j])
    else:
        exchange = (lambda j: x_ref.at[j]), (lambda j: head_place(lay, y_ref, j))
    begin_exchange(n, me, *exchange, *sems)
    attn_body(lay, phase, q_ref, k_ref, v_ref, o_ref, kt, v1, m_s, acc_s)
    end_exchange(n, me, *exchange, *sems)


def attention(lay, phase, carry, q, k, v, x, y_shape):
    n, parts, runs, run_rows, ph, span = lay
    rows, total = q.shape[0], k.shape[0]
    bq = math.gcd(rows, 1024)
    vmem = pl.BlockSpec(memory_space=pltpu.VMEM)
    return pl.pallas_call(
        functools.partial(attn_kernel, lay, phase, carry),
        in_specs=[vmem, vmem, vmem, pl.BlockSpec(memory_space=pl.ANY)],
        out_specs=[vmem, vmem],
        out_shape=[
            jax.ShapeDtypeStruct((rows, HD), jnp.bfloat16),
            jax.ShapeDtypeStruct(y_shape, jnp.bfloat16),
        ],
        scratch_shapes=[
            pltpu.VMEM((2 * HD, total), jnp.bfloat16),
            pltpu.VMEM((total, 2 * HD), jnp.bfloat16),
            pltpu.VMEM((bq, HD), jnp.float32),
            pltpu.VMEM((bq, 2 * HD), jnp.float32),
            pltpu.SemaphoreType.DMA((n,)),
            pltpu.SemaphoreType.DMA((n,)),
            pltpu.SemaphoreType.DMA,
        ],
        compiler_params=pltpu.CompilerParams(
            collective_id=2 + phase, has_side_effects=True, vmem_limit_bytes=50 * 2**20
        ),
    )(q, k, v, x)


MESH = pl.DeviceIdType.MESH


def greet(n, others=0):
    me = lax.axis_index("seq")
    barrier = pltpu.get_barrier_semaphore()

    @pl.loop(1, n)
    def _(d):
        pl.semaphore_signal(
            barrier, inc=1, device_id={"seq": lax.rem(me + d, n)}, device_id_type=MESH
        )

    pl.semaphore_wait(barrier, n - 1 + others)
    return me


def remote(src, dst, send, recv, peer):
    return pltpu.make_async_remote_copy(
        src_ref=src,
        dst_ref=dst,
        send_sem=send,
        recv_sem=recv,
        device_id={"seq": peer},
        device_id_type=MESH,
    )


def inbound(lay, dup, q_ref, k_ref, v_ref, q_o, k_o, v_o, send, recv, own, send2, recv2):
    n, parts, runs, run_rows, ph, span = lay
    me = greet(n)
    frac = span // dup

    def sources(j):
        q = query_source(lay, q_ref, 0, j)
        kv_rows = pl.ds(pl.multiple_of(lax.rem(j, dup) * frac, frac), frac)
        kv_cols = pl.ds(pl.multiple_of(j // dup * HD, HD), HD)
        return q, k_ref.at[kv_rows, kv_cols], v_ref.at[kv_rows, kv_cols]

    def places(owner, j):
        kv_rows = pl.ds(pl.multiple_of(lax.rem(j, dup) * frac, frac), frac)
        return q_o.at[owner], k_o.at[owner, kv_rows], v_o.at[owner, kv_rows]

    def copies(d):
        peer = lax.rem(me + d, n)
        pairs = zip(sources(peer), places(me, peer))
        return [remote(x, y, send.at[i, d], recv.at[i, d], peer) for i, (x, y) in enumerate(pairs)]

    @pl.loop(1, n)
    def _(d):
        for i in (1, 2, 0):
            copies(d)[i].start()

    local = [
        pltpu.make_async_copy(x, y, own.at[i])
        for i, (x, y) in enumerate(zip(sources(me), places(me, me)))
    ]
    for c in local:
        c.start()
    for c in local:
        c.wait()

    def arrived(i):
        @pl.loop(1, n)
        def _(d):
            owner = lax.rem(me + n - d, n)
            place = places(owner, me)[i]
            remote(place, place, send.at[i, d], recv.at[i, d], owner).wait_recv()

    arrived(1)
    arrived(2)
    base = me // dup * dup
    mine = lax.rem(me, dup)

    def shares(d):
        peer = base + lax.rem(mine + d, dup)
        rows = pl.ds(pl.multiple_of(mine * frac, frac), frac)
        return [
            remote(x.at[:, rows], x.at[:, rows], send2.at[i, d], recv2.at[i, d], peer)
            for i, x in enumerate((k_o, v_o))
        ]

    for d in range(1, dup):
        for c in shares(d):
            c.start()
    arrived(0)
    for d in range(1, dup):
        owner = lax.rem(mine + dup - d, dup)
        rows = pl.ds(pl.multiple_of(owner * frac, frac), frac)
        for i, x in enumerate((k_o, v_o)):
            place = x.at[:, rows]
            remote(place, place, send2.at[i, d], recv2.at[i, d], base + owner).wait_recv()
        for c in shares(d):
            c.wait_send()

    @pl.loop(1, n)
    def _(d):
        for c in copies(d):
            c.wait_send()


def gather_heads(lay, q, k, v, dup):
    n, parts, runs, run_rows, ph, span = lay
    any_space = pl.BlockSpec(memory_space=pl.ANY)
    vmem = pl.BlockSpec(memory_space=pltpu.VMEM)
    return pl.pallas_call(
        functools.partial(inbound, lay, dup),
        in_specs=[any_space] * 3,
        out_specs=[vmem] * 3,
        out_shape=[
            jax.ShapeDtypeStruct((n, runs, ph, HD), jnp.bfloat16),
            jax.ShapeDtypeStruct((n, span, HD), jnp.bfloat16),
            jax.ShapeDtypeStruct((n, span, HD), jnp.bfloat16),
        ],
        scratch_shapes=[
            pltpu.SemaphoreType.DMA((3, n)),
            pltpu.SemaphoreType.DMA((3, n)),
            pltpu.SemaphoreType.DMA((3,)),
            pltpu.SemaphoreType.DMA((2, dup)),
            pltpu.SemaphoreType.DMA((2, dup)),
        ],
        compiler_params=pltpu.CompilerParams(
            collective_id=0, has_side_effects=True, vmem_limit_bytes=40 * 2**20
        ),
    )(q, k, v)


def begin_exchange(n, me, source, place, send, recv, own):
    @pl.loop(1, n)
    def _(d):
        peer = lax.rem(me + d, n)
        remote(source(peer), place(me), send.at[d], recv.at[d], peer).start()

    pltpu.make_async_copy(source(me), place(me), own).start()


def end_exchange(n, me, source, place, send, recv, own):
    pltpu.make_async_copy(source(me), place(me), own).wait()

    @pl.loop(1, n)
    def _(d):
        owner = lax.rem(me + n - d, n)
        peer = lax.rem(me + d, n)
        there = place(owner)
        remote(there, there, send.at[d], recv.at[d], owner).wait_recv()
        remote(source(peer), place(me), send.at[d], recv.at[d], peer).wait_send()


def outbound(lay, heads, x_ref, t_ref, o_ref, g_ref, send, recv, own, send_x, recv_x):
    n = lay[0]
    mine = lax.axis_index("head")
    barrier = pltpu.get_barrier_semaphore()
    for k in range(1, heads):
        pl.semaphore_signal(
            barrier, inc=1, device_id={"head": lax.rem(mine + k, heads)}, device_id_type=MESH
        )
    me = greet(n, heads - 1)

    def term(k):
        return pltpu.make_async_remote_copy(
            src_ref=t_ref.at[k - 1],
            dst_ref=g_ref.at[k - 1],
            send_sem=send_x.at[k],
            recv_sem=recv_x.at[k],
            device_id={"head": lax.rem(mine + k, heads)},
            device_id_type=MESH,
        )

    exchange = (lambda j: x_ref.at[j]), (lambda j: head_place(lay, o_ref, j))
    for k in range(1, heads):
        term(k).start()
    begin_exchange(n, me, *exchange, send, recv, own)
    end_exchange(n, me, *exchange, send, recv, own)
    for k in range(1, heads):
        term(k).wait()


def return_heads(lay, x, shape, terms):
    n = lay[0]
    heads = lax.axis_size("head")
    space = pl.BlockSpec(memory_space=pl.ANY)
    return pl.pallas_call(
        functools.partial(outbound, lay, heads),
        in_specs=[space, space],
        out_specs=[pl.BlockSpec(memory_space=pltpu.VMEM), space],
        out_shape=[
            jax.ShapeDtypeStruct(shape, jnp.bfloat16),
            jax.ShapeDtypeStruct(terms.shape, jnp.bfloat16),
        ],
        scratch_shapes=[
            pltpu.SemaphoreType.DMA((n,)),
            pltpu.SemaphoreType.DMA((n,)),
            pltpu.SemaphoreType.DMA,
            pltpu.SemaphoreType.DMA((heads,)),
            pltpu.SemaphoreType.DMA((heads,)),
        ],
        compiler_params=pltpu.CompilerParams(
            collective_id=1, has_side_effects=True, vmem_limit_bytes=40 * 2**20
        ),
    )(x, terms)


def product(attended, out_weight, columns):
    y = jnp.dot(attended, out_weight[:, columns], preferred_element_type=jnp.float32)
    return lax.optimization_barrier(y.astype(jnp.bfloat16))


def rows_for(y, shift):
    heads = lax.axis_size("head")
    rows = y.shape[0] // heads
    dest = lax.rem(lax.axis_index("head") + shift, heads)
    return lax.dynamic_slice_in_dim(y, dest * rows, rows, 0)


def finish(y, got):
    total = rows_for(y, 0).astype(jnp.float32)
    for term in got:
        total = total + term.astype(jnp.float32)
    return total.astype(jnp.bfloat16)


def project_last(attended, out_weight, chunks):
    heads = lax.axis_size("head")
    step = out_weight.shape[1] // chunks
    ys = [product(attended, out_weight, slice(c * step, (c + 1) * step)) for c in range(chunks)]
    received = [
        [
            lax.ppermute(rows_for(y, k), "head", [(i, (i + k) % heads) for i in range(heads)])
            for k in range(1, heads)
        ]
        for y in ys
    ]
    return jnp.concatenate([finish(y, got) for y, got in zip(ys, received)], axis=1)


def per_device(queries, key_rows, values, out_weight):
    n = lax.axis_size("seq")
    heads = lax.axis_size("head")
    span = queries.shape[0]
    qh = queries.shape[1] // HD
    kvh = key_rows.shape[1] // HD
    parts = n // qh
    runs = max(1, heads // parts)
    groups = parts * runs
    run_rows = span // groups
    phases = 2
    ph = run_rows // phases
    lay = (n, parts, runs, run_rows, ph, span)
    columns = out_weight.shape[1]
    chunks = 6 if columns % (6 * HD) == 0 else 1
    grid = queries.reshape(groups, run_rows, qh * HD)
    q0, k, v = gather_heads(lay, grid, key_rows, values, n // kvh)
    k = k.reshape(n * span, HD)
    v = v.reshape(n * span, HD)
    own = (n, runs, ph, HD)
    back = (groups, ph, qh * HD)
    out0, q1 = attention(lay, 0, "queries", q0.reshape(-1, HD), k, v, grid, own)
    out1, att0 = attention(lay, 1, "heads", q1.reshape(-1, HD), k, v, out0.reshape(own), back)
    att0 = att0.reshape(groups * ph, qh * HD)
    y0 = product(att0, out_weight, slice(0, columns))
    terms = jnp.stack([rows_for(y0, k) for k in range(1, heads)])
    att1, got = return_heads(lay, out1.reshape(own), back, terms)
    second = project_last(att1.reshape(groups * ph, qh * HD), out_weight, chunks)
    first = finish(y0, [got[k] for k in range(heads - 1)])
    ends = [x.reshape(groups // heads, 1, ph, columns) for x in (first, second)]
    return jnp.concatenate(ends, axis=1).reshape(span // heads, columns)


def solution(mesh):
    placed = (P("seq", "head"), P("seq", "head"), P("seq", "head"), P("head", None))
    return jax.shard_map(
        per_device, mesh=mesh, in_specs=placed, out_specs=P(("seq", "head"), None), check_vma=False
    )
```
